32 devices in a mesh: parts: 2 (over x), ctx: 16 (over z, y, core).
Axes of the slice: x: 2, y: 2, z: 4, core: 2. Of those that a mesh axis runs over, the one named last changes fastest.
Arguments:
- queries: bfloat16 [256, 8192], P(('parts', 'ctx')), parts along dimension 0, may hold values from -24 to 24
- steer_ids: int32 [256], P(('parts', 'ctx')), parts along dimension 0, may hold values from 0 to 15
- steer_table: bfloat16 [16, 8192], replicated, may hold values from -3 to 3
- kv: bfloat16 [2, 32768, 1024], P(None, ('parts', 'ctx')), parts along dimension 1, may hold values from -4 to 4
- blocks: int32 [4, 128], P('parts'), parts along dimension 0, may hold values from 0 to 255, as said below
- w_out: bfloat16 [8192, 8192], P('ctx'), may hold values from -0.0625 to 0.0625
Outputs:
- projected: bfloat16 [256, 8192], P(('parts', 'ctx')), parts along dimension 0
The draws below stay inside these ranges and needn't reach their ends.
There are 2 independent parts, one for each index of `parts`. The reference program is written for one: setup_inputs(seed, part) draws one part's arguments, and reference() takes and returns one part's arrays. A program takes and returns all parts, laid end to end along the dimension named above; an argument that names none is the same for every part. Nothing has to cross between parts.
Inputs may be any that keep to these rules, and one draw needn't show every extreme that they name: Each row lists 128 distinct key blocks and always includes block 0 and block 255.
All inputs are finite; a program needn't handle non-finite values.
Results may differ from the reference program's by a relative error of at most 0.0066.
Values may be sent and summed in bfloat16 or wider, within the bound.
No kernel may reach another device: no remote copies, remote signals or barrier semaphores. Data moves between devices by JAX's collectives and lax.ppermute only.
A program may use at most 64 MiB of HBM per device.

```python
import jax
import jax.numpy as jnp
from jax import lax

HEADS = 64
KV_HEADS = 8
HEAD = 128
D = 8192
QUERIES = 128
CTX_DEV = 1024
BLOCK = 64
STEERS = 16
CONTEXT = 16384
BLOCKS_DEV = 16
KEY_BLOCKS = 256
QUERY_BLOCKS = 2
KEEP = 128
N_CTX = 16


def draw_queries(key, part):
    inner_key = jax.random.fold_in(key, 11)
    base_draw = jnp.clip(jax.random.normal(inner_key, (QUERIES, D), jnp.float32), -4.0, 4.0)
    shaped = base_draw.reshape(QUERIES, HEADS, HEAD)
    return shaped.reshape(QUERIES, D).astype(jnp.bfloat16)


def draw_kv(key, part):
    inner_key = jax.random.fold_in(key, 23)
    values_all = jnp.clip(jax.random.normal(inner_key, (2, CONTEXT, KV_HEADS * HEAD), jnp.float32), -4.0, 4.0)
    return values_all.astype(jnp.bfloat16)


def draw_blocks(key, part):
    random_part = jax.random.randint(jax.random.fold_in(key, 31), (QUERY_BLOCKS, KEY_BLOCKS), 0, 1024)
    hot_shards = jax.random.randint(jax.random.fold_in(key, 32), (KEY_BLOCKS // BLOCKS_DEV,), 0, 3) * 512
    hot_blocks = jnp.repeat(hot_shards, BLOCKS_DEV)
    forced = jnp.zeros((KEY_BLOCKS,), jnp.int32).at[0].set(4096).at[KEY_BLOCKS - 1].set(4096)
    ranked = (random_part + hot_blocks[None, :] + forced[None, :]) * KEY_BLOCKS + jnp.arange(KEY_BLOCKS, dtype=jnp.int32)[None, :]
    top_values, chosen = lax.top_k(ranked, KEEP)
    return chosen.astype(jnp.int32)


def touch_ends(values, key, least, largest):
    shape = values.shape
    index_at = [jax.random.randint(jax.random.fold_in(key, axis), (), 0, shape[axis]) for axis in range(len(shape))]
    values = values.at[tuple(index_at)].set(least)
    longest = shape.index(max(shape))
    index_at[longest] = (index_at[longest] + 1) % shape[longest]
    return values.at[tuple(index_at)].set(largest)


def shard_levels(stream_key, dims, shards, smallest, high):
    loudness = 1.0
    for axis_at, blocks in shards:
        draws = jax.random.uniform(jax.random.fold_in(jax.random.fold_in(stream_key, 6), axis_at), (blocks,), jnp.float32, smallest / len(shards), high / len(shards))
        loudness = loudness * jnp.repeat(jnp.exp(draws), dims[axis_at] // blocks).reshape((-1,) + (1,) * (len(dims) - 1 - axis_at))
    return loudness


def normal_values(rng, shape, deviation, most, shards=(), kind=jnp.bfloat16):
    entries = jax.random.normal(rng, shape, jnp.float32) * deviation
    if len(shards) > 0:
        entries = shard_levels(rng, shape, shards, -0.22, 0.18) * entries
    return jnp.clip(entries, min=-most, max=most).astype(kind)


def setup_inputs(seed: int = 0, part: int = 0) -> dict:
    streams_of = jax.random.split(jax.random.key(seed), 7)
    part_splits = jax.random.split(jax.random.fold_in(streams_of[6], part), 7)
    return {
        "queries": draw_queries(jax.random.fold_in(jax.random.fold_in(streams_of[6], part), 71), part),
        "steer_ids": touch_ends(jax.random.randint(part_splits[1], (QUERIES,), 0, STEERS), jax.random.fold_in(part_splits[1], 1), 0, STEERS - 1).astype(jnp.int32),
        "steer_table": normal_values(streams_of[2], (STEERS, D), 0.5, 3.0),
        "kv": draw_kv(jax.random.fold_in(jax.random.fold_in(streams_of[6], part), 71), part),
        "blocks": draw_blocks(jax.random.fold_in(jax.random.fold_in(streams_of[6], part), 71), part),
        "w_out": normal_values(streams_of[5], (D, D), D ** -0.5, 0.0625, ((0, 16),)),
    }


def apply_steer(queries, steer_ids, steer_table):
    lookup_ids = jnp.arange(steer_table.shape[0], dtype=jnp.int32)
    one_hot = (steer_ids[:, None] == lookup_ids[None, :]).astype(jnp.bfloat16)
    lookup = jnp.dot(one_hot, steer_table, preferred_element_type=jnp.float32)
    return (queries.astype(jnp.float32) + lookup).astype(jnp.bfloat16)


def local_keep(blocks, first_block, block_count, query_count):
    block_ids = first_block + jnp.arange(block_count, dtype=jnp.int32)
    hits = jnp.any(blocks[:, :, None] == block_ids[None, None, :], axis=1)
    full = jnp.broadcast_to(hits[:, None, :, None], (query_count // BLOCK, BLOCK, block_count, BLOCK))
    return full.reshape(query_count, block_count * BLOCK)


def group_attend(q_rows, k_rows, v_rows, keep_rows):
    scores = lax.dot_general(q_rows, k_rows, (((1,), (1,)), ((), ())), preferred_element_type=jnp.float32)
    scores = scores * (HEAD ** -0.5)
    masked = jnp.where(keep_rows, scores, jnp.float32(-1e30))
    row_peak = jnp.max(masked, axis=1)
    weights = jnp.where(keep_rows, jnp.exp(masked - row_peak[:, None]), jnp.float32(0.0))
    row_total = jnp.sum(weights, axis=1)
    probs = weights.astype(jnp.bfloat16)
    partial_out = jnp.dot(probs, v_rows, preferred_element_type=jnp.float32)
    return row_peak, row_total, partial_out


def partial_attention(steered, kv_piece, keep_mask):
    query_count = steered.shape[0]
    ctx_count = kv_piece.shape[1]
    group_size = HEADS // KV_HEADS
    q_groups = steered.reshape(query_count, KV_HEADS, group_size, HEAD).transpose(1, 2, 0, 3)
    q_groups = q_groups.reshape(KV_HEADS, group_size * query_count, HEAD)
    k_groups = kv_piece[0].reshape(ctx_count, KV_HEADS, HEAD).transpose(1, 0, 2)
    v_groups = kv_piece[1].reshape(ctx_count, KV_HEADS, HEAD).transpose(1, 0, 2)
    keep_rows = jnp.tile(keep_mask, (group_size, 1))

    def one_group(triple):
        return group_attend(triple[0], triple[1], triple[2], keep_rows)

    peaks, totals, outs = lax.map(one_group, (q_groups, k_groups, v_groups))
    peaks = peaks.reshape(KV_HEADS, group_size, query_count).transpose(2, 0, 1).reshape(query_count, HEADS)
    totals = totals.reshape(KV_HEADS, group_size, query_count).transpose(2, 0, 1).reshape(query_count, HEADS)
    outs = outs.reshape(KV_HEADS, group_size, query_count, HEAD).transpose(2, 0, 1, 3).reshape(query_count, HEADS * HEAD)
    return peaks, totals, outs


def reference(queries, steer_ids, steer_table, kv, blocks, w_out):
    steered = apply_steer(queries, steer_ids, steer_table)
    query_count = steered.shape[0]

    def visit(carry, shard_index):
        run_max, run_den, run_num = carry
        kv_piece = lax.dynamic_slice_in_dim(kv, shard_index * CTX_DEV, CTX_DEV, 1)
        keep_mask = local_keep(blocks, shard_index * BLOCKS_DEV, BLOCKS_DEV, query_count)
        peaks, totals, outs = partial_attention(steered, kv_piece, keep_mask)
        new_max = jnp.maximum(run_max, peaks)
        old_scale = jnp.exp(run_max - new_max)
        new_scale = jnp.exp(peaks - new_max)
        run_den = run_den * old_scale + totals * new_scale
        run_num = run_num * jnp.repeat(old_scale, HEAD, axis=1) + outs * jnp.repeat(new_scale, HEAD, axis=1)
        return (new_max, run_den, run_num), None

    start = (jnp.full((query_count, HEADS), -1e30, jnp.float32), jnp.zeros((query_count, HEADS), jnp.float32), jnp.zeros((query_count, HEADS * HEAD), jnp.float32))
    final, unused = lax.scan(visit, start, jnp.arange(N_CTX, dtype=jnp.int32))
    attended = (final[2] / jnp.repeat(final[1], HEAD, axis=1)).astype(jnp.bfloat16)
    return jnp.dot(attended, w_out, preferred_element_type=jnp.float32).astype(jnp.bfloat16)
```

```python
import jax
import jax.numpy as jnp
from jax import lax
from jax.experimental import pallas as pl
from jax.experimental.pallas import tpu as pltpu
from jax.sharding import PartitionSpec as P

HEADS = 64
KV_HEADS = 8
HEAD = 128
D = 8192
BLOCK = 64


def apply_steer(queries, steer_ids, steer_table):
    lookup_ids = jnp.arange(steer_table.shape[0], dtype=jnp.int32)
    one_hot = (steer_ids[:, None] == lookup_ids[None, :]).astype(jnp.bfloat16)
    lookup = jnp.dot(one_hot, steer_table, preferred_element_type=jnp.float32)
    return (queries.astype(jnp.float32) + lookup).astype(jnp.bfloat16)


def local_keep(blocks, first_block, block_count, query_count):
    block_ids = first_block + jnp.arange(block_count, dtype=jnp.int32)
    hits = jnp.any(blocks[:, :, None] == block_ids[None, None, :], axis=1)
    full = jnp.broadcast_to(
        hits[:, None, :, None], (query_count // BLOCK, BLOCK, block_count, BLOCK)
    )
    return full.reshape(query_count, block_count * BLOCK)


def group_attend(q_rows, k_rows, v_rows, keep_rows):
    scores = lax.dot_general(
        q_rows, k_rows, (((1,), (1,)), ((), ())), preferred_element_type=jnp.float32
    )
    scores = scores * HEAD ** (-0.5)
    masked = jnp.where(keep_rows, scores, jnp.float32(-1e30))
    row_peak = jnp.max(masked, axis=1)
    weights = jnp.where(keep_rows, jnp.exp(masked - row_peak[:, None]), jnp.float32(0.0))
    row_total = jnp.sum(weights, axis=1)
    probs = weights.astype(jnp.bfloat16)
    partial_out = jnp.dot(probs, v_rows, preferred_element_type=jnp.float32)
    return (row_peak, row_total, partial_out)


def partial_attention(steered, kv_piece, keep_mask):
    query_count = steered.shape[0]
    ctx_count = kv_piece.shape[1]
    group_size = HEADS // KV_HEADS
    q_groups = steered.reshape(query_count, KV_HEADS, group_size, HEAD).transpose(1, 2, 0, 3)
    q_groups = q_groups.reshape(KV_HEADS, group_size * query_count, HEAD)
    k_groups = kv_piece[0].reshape(ctx_count, KV_HEADS, HEAD).transpose(1, 0, 2)
    v_groups = kv_piece[1].reshape(ctx_count, KV_HEADS, HEAD).transpose(1, 0, 2)
    keep_rows = jnp.tile(keep_mask, (group_size, 1))

    def one_group(triple):
        return group_attend(triple[0], triple[1], triple[2], keep_rows)

    peaks, totals, outs = lax.map(one_group, (q_groups, k_groups, v_groups))
    peaks = (
        peaks.reshape(KV_HEADS, group_size, query_count)
        .transpose(2, 0, 1)
        .reshape(query_count, HEADS)
    )
    totals = (
        totals.reshape(KV_HEADS, group_size, query_count)
        .transpose(2, 0, 1)
        .reshape(query_count, HEADS)
    )
    outs = (
        outs.reshape(KV_HEADS, group_size, query_count, HEAD)
        .transpose(2, 0, 1, 3)
        .reshape(query_count, HEADS * HEAD)
    )
    return (peaks, totals, outs)


def per_device(queries, steer_ids, steer_table, kv, blocks, w_out):
    steered_local = apply_steer(queries, steer_ids, steer_table)
    steered = lax.all_gather(steered_local, "ctx", axis=0, tiled=True)
    shard_count = lax.axis_size("ctx")
    my_index = lax.axis_index("ctx")
    query_count = steered.shape[0]
    block_count = kv.shape[1] // BLOCK
    keep_mask = local_keep(blocks, my_index * block_count, block_count, query_count)
    peaks, totals, outs = partial_attention(steered, kv, keep_mask)
    stat_width = max(HEADS, shard_count)
    per_entry = D // stat_width
    col_count = D // shard_count

    def spread(values):
        return jnp.repeat(values, stat_width // HEADS, axis=1)

    got_num, got_max, got_den = (
        lax.all_to_all(outs, "ctx", split_axis=1, concat_axis=0, tiled=True),
        lax.all_to_all(spread(peaks), "ctx", split_axis=1, concat_axis=0, tiled=True),
        lax.all_to_all(spread(totals), "ctx", split_axis=1, concat_axis=0, tiled=True),
    )
    got_num = got_num.reshape(shard_count, query_count, col_count)
    got_max = got_max.reshape(shard_count, query_count, stat_width // shard_count)
    got_den = got_den.reshape(shard_count, query_count, stat_width // shard_count)
    overall = jnp.max(got_max, axis=0)
    scales = jnp.exp(got_max - overall[None])
    denominator = jnp.sum(scales * got_den, axis=0)
    numerator = jnp.sum(jnp.repeat(scales, per_entry, axis=2) * got_num, axis=0)
    attended = (numerator / jnp.repeat(denominator, per_entry, axis=1)).astype(jnp.bfloat16)
    return lax.psum_scatter(
        jnp.dot(attended, w_out, preferred_element_type=jnp.float32),
        "ctx",
        scatter_dimension=0,
        tiled=True,
    ).astype(jnp.bfloat16)


NONE = -1e30
LOG2E = 1.4426950408889634
STAT_ROWS = 16


def attend_kernel(heads, tile, order, *refs):
    n_blocks = order.shape[0]
    q_blocks = refs[:n_blocks]
    k_own, k_far, v_own, v_far, keep, out, q_all, scores = refs[n_blocks:]
    group = pl.program_id(0)
    block_rows = q_blocks[0].shape[0]
    rows = n_blocks * block_rows
    ctx = k_own.shape[1]
    per_tile = tile // BLOCK
    to_log2 = HEAD ** (-0.5) * LOG2E

    for at in range(n_blocks):
        q_all[order[at]] = q_blocks[at][...]

    pieces = [(k_own, v_own, 0, t) for t in range(ctx // tile)]
    pieces += [(k_far, v_far, ctx // BLOCK, t) for t in range(ctx // tile)]
    stats = [[], [], []]
    for pair in range(heads // 2):
        q_pair = jnp.concatenate(
            [
                q_all[:, :, (2 * pair + j) * HEAD : (2 * pair + j + 1) * HEAD].reshape(rows, HEAD)
                for j in range(2)
            ],
            axis=0,
        )
        peak = jnp.full((1, 2 * rows), NONE, jnp.float32)
        for at, (k_ref, v_ref, first, t) in enumerate(pieces):
            piece = lax.dot_general(
                k_ref[0, t * tile : (t + 1) * tile, :],
                q_pair,
                (((1,), (1,)), ((), ())),
                preferred_element_type=jnp.float32,
            )
            scores[pair, at * tile : (at + 1) * tile, :] = piece
            for b in range(per_tile):
                kept = keep[pl.ds(first + t * per_tile + b, 1), :]
                best = jnp.max(piece[b * BLOCK : (b + 1) * BLOCK, :], axis=0, keepdims=True)
                peak = jnp.maximum(peak, jnp.where(kept > 0.0, best * to_log2, NONE))
        peak_sent = peak.astype(jnp.bfloat16)
        peak = peak_sent.astype(jnp.float32)
        total = jnp.zeros((8, 2 * rows), jnp.float32)
        value = jnp.zeros((HEAD, 2 * rows), jnp.float32)
        for at, (k_ref, v_ref, first, t) in enumerate(pieces):
            probs = []
            for b in range(per_tile):
                kept = keep[pl.ds(first + t * per_tile + b, 1), :]
                shift = jnp.where(kept > 0.0, peak, -NONE)
                low = at * tile + b * BLOCK
                weights = jnp.exp2(scores[pair, low : low + BLOCK, :] * to_log2 - shift)
                total = total + jnp.sum(weights.reshape(BLOCK // 8, 8, 2 * rows), axis=0)
                probs.append(weights.astype(jnp.bfloat16))
            value = value + jnp.dot(
                v_ref[:, t * tile : (t + 1) * tile],
                jnp.concatenate(probs, axis=0),
                preferred_element_type=jnp.float32,
            )
        total = jnp.sum(total, axis=0, keepdims=True)
        total_high = total.astype(jnp.bfloat16).astype(jnp.float32)
        total_low = total - total_high
        for j in range(2):
            half = slice(j * rows, (j + 1) * rows)
            low = (2 * pair + j) * HEAD
            out[0, low : low + HEAD, :] = value[:, half].astype(jnp.bfloat16)
            stats[0].append(peak[:, half])
            stats[1].append(total_high[:, half])
            stats[2].append(total_low[:, half])
    flat = stats[0] + stats[1] + stats[2]
    flat += [jnp.zeros_like(flat[0])] * (STAT_ROWS - len(flat))
    out[0, heads * HEAD :, :] = jnp.concatenate(flat, axis=0).astype(jnp.bfloat16)


def attend(q_blocks, order, kv, kv_far, v_turned, v_far_turned, keep, heads, tile=256):
    block_rows = q_blocks[0].shape[0]
    rows = block_rows * len(q_blocks)
    ctx = kv.shape[1]
    width = heads * HEAD
    length = width + STAT_ROWS

    def column(g, order_ref):
        return (0, g)

    return pl.pallas_call(
        lambda *refs: attend_kernel(heads, tile, *refs),
        grid_spec=pltpu.PrefetchScalarGridSpec(
            num_scalar_prefetch=1,
            grid=(KV_HEADS,),
            in_specs=[pl.BlockSpec((block_rows, width), column) for _ in q_blocks]
            + [
                pl.BlockSpec((1, ctx, HEAD), lambda g, o: (0, 0, g)),
                pl.BlockSpec((1, ctx, HEAD), lambda g, o: (0, 0, g)),
                pl.BlockSpec((HEAD, ctx), lambda g, o: (g, 0)),
                pl.BlockSpec((HEAD, ctx), lambda g, o: (g, 0)),
                pl.BlockSpec(keep.shape, lambda g, o: (0, 0)),
            ],
            out_specs=pl.BlockSpec((1, length, rows), lambda g, o: (g, 0, 0)),
            scratch_shapes=[
                pltpu.VMEM((len(q_blocks), block_rows, width), jnp.bfloat16),
                pltpu.VMEM((heads // 2, 2 * ctx, 2 * rows), jnp.float32),
            ],
        ),
        out_shape=jax.ShapeDtypeStruct((KV_HEADS, length, rows), jnp.bfloat16),
        compiler_params=pltpu.CompilerParams(
            dimension_semantics=("arbitrary",), vmem_limit_bytes=40 * 1024 * 1024
        ),
        cost_estimate=pl.CostEstimate(
            flops=4 * rows * KV_HEADS * width * 2 * ctx,
            bytes_accessed=8 * ctx * KV_HEADS * HEAD,
            transcendentals=rows * KV_HEADS * heads * 2 * ctx,
        ),
        name="attend",
    )(order, *q_blocks, kv, kv_far, v_turned, v_far_turned, keep)


def project_kernel(heads, core, parts, w_ref, kept, sent, attended):
    @pl.when(pl.program_id(0) == 0)
    def _():
        stats = parts[:, heads * HEAD :, :].astype(jnp.float32)
        peaks = stats[:, :heads, :]
        totals = stats[:, heads : 2 * heads, :] + stats[:, 2 * heads : 3 * heads, :]
        scales = jnp.exp2(peaks - jnp.max(peaks, axis=0, keepdims=True))
        below = jnp.sum(scales * totals, axis=0)
        for h in range(heads):
            above = jnp.zeros((HEAD, parts.shape[2]), jnp.float32)
            for s in range(parts.shape[0]):
                piece = parts[s, h * HEAD : (h + 1) * HEAD, :].astype(jnp.float32)
                above = above + piece * scales[s, h : h + 1, :]
            mean = above / below[h : h + 1, :]
            attended[:, h * HEAD : (h + 1) * HEAD] = mean.T.astype(jnp.bfloat16)

    full = jnp.dot(attended[...], w_ref[...], preferred_element_type=jnp.float32)
    per_dev, tile = kept.shape[1], kept.shape[2]
    full = full.reshape(kept.shape[0], 2, per_dev, tile)
    first = core[0] == 0
    kept[...] = jnp.where(first, full[:, 0], full[:, 1])
    away = jnp.where(first, full[:, 1], full[:, 0])
    sent[...] = away.reshape(kept.shape[0] * per_dev, tile).astype(jnp.bfloat16)


def project(parts, core, w_out, heads, per_dev, tile=1024):
    shards, length, rows = parts.shape
    chips = rows // (2 * per_dev)
    return pl.pallas_call(
        lambda *refs: project_kernel(heads, *refs),
        grid_spec=pltpu.PrefetchScalarGridSpec(
            num_scalar_prefetch=1,
            grid=(D // tile,),
            in_specs=[
                pl.BlockSpec((shards, length, rows), lambda j, c: (0, 0, 0)),
                pl.BlockSpec((heads * HEAD, tile), lambda j, c: (0, j)),
            ],
            out_specs=[
                pl.BlockSpec((chips, per_dev, tile), lambda j, c: (0, 0, j)),
                pl.BlockSpec((chips * per_dev, tile), lambda j, c: (0, j)),
            ],
            scratch_shapes=[pltpu.VMEM((rows, heads * HEAD), jnp.bfloat16)],
        ),
        out_shape=[
            jax.ShapeDtypeStruct((chips, per_dev, D), jnp.float32),
            jax.ShapeDtypeStruct((chips * per_dev, D), jnp.bfloat16),
        ],
        compiler_params=pltpu.CompilerParams(dimension_semantics=("arbitrary",)),
        cost_estimate=pl.CostEstimate(
            flops=2 * rows * heads * HEAD * D, bytes_accessed=3 * heads * HEAD * D, transcendentals=0
        ),
        name="project",
    )(core, parts, w_out)


def ring_of(chips):
    return [c for c in range(0, chips, 2)] + [c for c in range(chips - 1, 0, -2)]


def paired_device(queries, steer_ids, steer_table, kv, blocks, w_out):
    n = lax.axis_size("ctx")
    me = lax.axis_index("ctx")
    chips = n // 2
    core = me % 2
    chip = me // 2
    per_dev = queries.shape[0]
    rows = per_dev * n
    width = D // n
    heads = width // HEAD
    swap = [(i, i ^ 1) for i in range(n)]
    evens_odds = [[2 * c for c in range(chips)], [2 * c + 1 for c in range(chips)]]
    ring = ring_of(chips)

    steered = apply_steer(queries, steer_ids, steer_table)
    halves = steered.reshape(per_dev, chips, 2, width)
    mine = jnp.where(core == 0, halves[:, :, 0], halves[:, :, 1]).reshape(per_dev, D // 2)
    other = jnp.where(core == 0, halves[:, :, 1], halves[:, :, 0]).reshape(per_dev, D // 2)
    theirs = lax.ppermute(other, "ctx", swap)
    block = jnp.concatenate(
        [jnp.where(core == 0, mine, theirs), jnp.where(core == 0, theirs, mine)], axis=0
    )
    kv_far = lax.ppermute(kv, "ctx", swap)

    def hop(step):
        return [
            (2 * ring[p] + c, 2 * ring[(p + step) % chips] + c) for p in range(chips) for c in range(2)
        ]

    found, offsets = [block], [0]
    ahead, behind = block, block
    for s in range(1, chips // 2 + 1):
        ahead = lax.ppermute(ahead, "ctx", hop(1))
        found.append(ahead)
        offsets.append(-s)
        if s < chips - s:
            behind = lax.ppermute(behind, "ctx", hop(-1))
            found.append(behind)
            offsets.append(s)
    ring_array = jnp.array(ring, jnp.int32)
    place_array = jnp.array([ring.index(c) for c in range(chips)], jnp.int32)
    place = place_array[chip]
    order = ring_array[(place + jnp.array(offsets, jnp.int32)) % chips]

    v_turned = kv[1].T
    v_far_turned = kv_far[1].T
    block_count = kv.shape[1] // BLOCK
    ids = jnp.arange(block_count, dtype=jnp.int32)
    ids = jnp.concatenate([me * block_count + ids, (me ^ 1) * block_count + ids])
    hits = jnp.any(blocks[:, None, :] == ids[None, :, None], axis=2)
    keep = jnp.repeat(hits.T.astype(jnp.float32), BLOCK, axis=1)
    keep = jnp.concatenate([keep, keep], axis=1)

    message = attend(found, order, kv, kv_far, v_turned, v_far_turned, keep, heads)
    parts = lax.all_to_all(
        message, "ctx", split_axis=0, concat_axis=0, axis_index_groups=evens_odds, tiled=True
    )
    kept, sent = project(parts, core.reshape(1), w_out, heads, per_dev)
    got = lax.ppermute(sent, "ctx", swap)
    summed = (kept.reshape(chips * per_dev, D) + got.astype(jnp.float32)).astype(jnp.bfloat16)
    pieces = lax.all_to_all(
        summed, "ctx", split_axis=0, concat_axis=0, axis_index_groups=evens_odds, tiled=True
    )
    pieces = pieces.reshape(chips, per_dev, D).astype(jnp.float32)
    return jnp.sum(pieces, axis=0).astype(jnp.bfloat16)


def solution(mesh):
    n = mesh.shape["ctx"]
    paired = n == 2 * KV_HEADS
    return jax.shard_map(
        paired_device if paired else per_device,
        mesh=mesh,
        in_specs=(
            P(("parts", "ctx"), None),
            P(("parts", "ctx")),
            P(),
            P(None, ("parts", "ctx"), None),
            P("parts", None),
            P("ctx", None),
        ),
        out_specs=P(("parts", "ctx"), None),
        check_vma=False,
    )
```

```python
import jax
import jax.numpy as jnp
from jax import lax
from jax.experimental import pallas as pl
from jax.experimental.pallas import tpu as pltpu
from jax.sharding import PartitionSpec as P

HEADS = 64
KV_HEADS = 8
HEAD = 128
D = 8192
BLOCK = 64


def apply_steer(queries, steer_ids, steer_table):
    lookup_ids = jnp.arange(steer_table.shape[0], dtype=jnp.int32)
    one_hot = (steer_ids[:, None] == lookup_ids[None, :]).astype(jnp.bfloat16)
    lookup = jnp.dot(one_hot, steer_table, preferred_element_type=jnp.float32)
    return (queries.astype(jnp.float32) + lookup).astype(jnp.bfloat16)


def local_keep(blocks, first_block, block_count, query_count):
    block_ids = first_block + jnp.arange(block_count, dtype=jnp.int32)
    hits = jnp.any(blocks[:, :, None] == block_ids[None, None, :], axis=1)
    full = jnp.broadcast_to(
        hits[:, None, :, None], (query_count // BLOCK, BLOCK, block_count, BLOCK)
    )
    return full.reshape(query_count, block_count * BLOCK)


def group_attend(q_rows, k_rows, v_rows, keep_rows):
    scores = lax.dot_general(
        q_rows, k_rows, (((1,), (1,)), ((), ())), preferred_element_type=jnp.float32
    )
    scores = scores * HEAD ** (-0.5)
    masked = jnp.where(keep_rows, scores, jnp.float32(-1e30))
    row_peak = jnp.max(masked, axis=1)
    weights = jnp.where(keep_rows, jnp.exp(masked - row_peak[:, None]), jnp.float32(0.0))
    row_total = jnp.sum(weights, axis=1)
    probs = weights.astype(jnp.bfloat16)
    partial_out = jnp.dot(probs, v_rows, preferred_element_type=jnp.float32)
    return (row_peak, row_total, partial_out)


def partial_attention(steered, kv_piece, keep_mask):
    query_count = steered.shape[0]
    ctx_count = kv_piece.shape[1]
    group_size = HEADS // KV_HEADS
    q_groups = steered.reshape(query_count, KV_HEADS, group_size, HEAD).transpose(1, 2, 0, 3)
    q_groups = q_groups.reshape(KV_HEADS, group_size * query_count, HEAD)
    k_groups = kv_piece[0].reshape(ctx_count, KV_HEADS, HEAD).transpose(1, 0, 2)
    v_groups = kv_piece[1].reshape(ctx_count, KV_HEADS, HEAD).transpose(1, 0, 2)
    keep_rows = jnp.tile(keep_mask, (group_size, 1))

    def one_group(triple):
        return group_attend(triple[0], triple[1], triple[2], keep_rows)

    peaks, totals, outs = lax.map(one_group, (q_groups, k_groups, v_groups))
    peaks = (
        peaks.reshape(KV_HEADS, group_size, query_count)
        .transpose(2, 0, 1)
        .reshape(query_count, HEADS)
    )
    totals = (
        totals.reshape(KV_HEADS, group_size, query_count)
        .transpose(2, 0, 1)
        .reshape(query_count, HEADS)
    )
    outs = (
        outs.reshape(KV_HEADS, group_size, query_count, HEAD)
        .transpose(2, 0, 1, 3)
        .reshape(query_count, HEADS * HEAD)
    )
    return (peaks, totals, outs)


def per_device(queries, steer_ids, steer_table, kv, blocks, w_out):
    steered_local = apply_steer(queries, steer_ids, steer_table)
    steered = lax.all_gather(steered_local, "ctx", axis=0, tiled=True)
    shard_count = lax.axis_size("ctx")
    my_index = lax.axis_index("ctx")
    query_count = steered.shape[0]
    block_count = kv.shape[1] // BLOCK
    keep_mask = local_keep(blocks, my_index * block_count, block_count, query_count)
    peaks, totals, outs = partial_attention(steered, kv, keep_mask)
    stat_width = max(HEADS, shard_count)
    per_entry = D // stat_width
    col_count = D // shard_count

    def spread(values):
        return jnp.repeat(values, stat_width // HEADS, axis=1)

    got_num, got_max, got_den = (
        lax.all_to_all(outs, "ctx", split_axis=1, concat_axis=0, tiled=True),
        lax.all_to_all(spread(peaks), "ctx", split_axis=1, concat_axis=0, tiled=True),
        lax.all_to_all(spread(totals), "ctx", split_axis=1, concat_axis=0, tiled=True),
    )
    got_num = got_num.reshape(shard_count, query_count, col_count)
    got_max = got_max.reshape(shard_count, query_count, stat_width // shard_count)
    got_den = got_den.reshape(shard_count, query_count, stat_width // shard_count)
    overall = jnp.max(got_max, axis=0)
    scales = jnp.exp(got_max - overall[None])
    denominator = jnp.sum(scales * got_den, axis=0)
    numerator = jnp.sum(jnp.repeat(scales, per_entry, axis=2) * got_num, axis=0)
    attended = (numerator / jnp.repeat(denominator, per_entry, axis=1)).astype(jnp.bfloat16)
    return lax.psum_scatter(
        jnp.dot(attended, w_out, preferred_element_type=jnp.float32),
        "ctx",
        scatter_dimension=0,
        tiled=True,
    ).astype(jnp.bfloat16)


NONE = -(2.0**100)
LOG2E = 1.4426950408889634
STAT_ROWS = 16
ATTEND_VMEM = 60 * 1024 * 1024


def pack_stats(peaks, totals):
    high = [t.astype(jnp.bfloat16).astype(jnp.float32) for t in totals]
    flat = peaks + high + [t - h for t, h in zip(totals, high)]
    flat += [jnp.zeros_like(flat[0])] * (STAT_ROWS - len(flat))
    return jnp.concatenate(flat, axis=0).astype(jnp.bfloat16)


def unpack_stats(stats, heads):
    stats = stats.astype(jnp.float32)
    return stats[:heads], stats[heads : 2 * heads] + stats[2 * heads : 3 * heads]


def attend_kernel(heads, tile, order, groups, *refs):
    n_blocks, count = order.shape[0], groups.shape[0]
    q_blocks = refs[: n_blocks * count]
    sources = refs[n_blocks * count : n_blocks * count + 2]
    keep = refs[n_blocks * count + 2]
    outs = refs[n_blocks * count + 3 : n_blocks * count + 3 + count]
    held, q_all, scores, acc, arrived = refs[n_blocks * count + 3 + count :]
    block_rows = q_blocks[0].shape[0]
    rows = n_blocks * block_rows
    lanes = heads * rows
    ctx = held.shape[1]
    key_blocks, per_tile = ctx // BLOCK, tile // BLOCK
    to_log2 = HEAD ** (-0.5) * LOG2E
    units = [(i, s) for i in range(count) for s in range(2)]

    def fetch(u, kind):
        i, s = units[u]
        column = pl.ds(pl.multiple_of(groups[i] * HEAD, HEAD), HEAD)
        at = 2 * u + kind
        return pltpu.make_async_copy(sources[s].at[kind, :, column], held.at[at], arrived.at[at])

    for u in range(len(units)):
        for kind in range(2):
            fetch(u, kind).start()
    for i in range(count):
        for at in range(n_blocks):
            for h in range(heads):
                q_all[i, h, order[at]] = q_blocks[i * n_blocks + at][:, h * HEAD : (h + 1) * HEAD]

    def score(u, t, peak):
        i, s = units[u]
        piece = lax.dot_general(
            held[2 * u, t * tile : (t + 1) * tile, :],
            q_all[i].reshape(lanes, HEAD),
            (((1,), (1,)), ((), ())),
            preferred_element_type=jnp.float32,
        )
        scores[u % 2, t * tile : (t + 1) * tile, :] = piece
        for b in range(per_tile):
            kept = keep[pl.ds(s * key_blocks + t * per_tile + b, 1), :]
            part = piece[b * BLOCK : (b + 1) * BLOCK, :].reshape(BLOCK // 8, 8, lanes)
            best = jnp.max(part, axis=0) * to_log2
            peak = jnp.maximum(peak, jnp.where(kept > 0.0, best, NONE))
        return peak

    def weigh(u, t, peak, total):
        s = units[u][1]
        probs = []
        for b in range(per_tile):
            kept = keep[pl.ds(s * key_blocks + t * per_tile + b, 1), :]
            shift = jnp.where(kept > 0.0, peak, -NONE)
            low = t * tile + b * BLOCK
            weights = jnp.exp2(scores[u % 2, low : low + BLOCK, :] * to_log2 - shift)
            total = total + jnp.sum(weights.reshape(BLOCK // 8, 8, lanes), axis=0)
            probs.append(weights.astype(jnp.bfloat16))
        fresh = jnp.dot(
            held[2 * u + 1, t * tile : (t + 1) * tile, :].T,
            jnp.concatenate(probs, axis=0),
            preferred_element_type=jnp.float32,
        )
        acc[s] = fresh if t == 0 else acc[s] + fresh
        return total

    tiles = range(ctx // tile)
    lowest = jnp.full((8, lanes), NONE, jnp.float32)
    fetch(0, 0).wait()
    peak = lowest
    for t in tiles:
        peak = score(0, t, peak)
    peaks, totals = [], []
    for u, (i, s) in enumerate(units):
        row = jnp.max(peak, axis=0, keepdims=True)
        total = jnp.zeros((8, lanes), jnp.float32)
        fetch(u, 1).wait()
        peak = lowest
        if u + 1 < len(units):
            fetch(u + 1, 0).wait()
        for t in tiles:
            if u + 1 < len(units):
                peak = score(u + 1, t, peak)
            total = weigh(u, t, row, total)
        peaks.append(row)
        totals.append(jnp.sum(total, axis=0, keepdims=True))
        if s == 1:
            top = jnp.maximum(peaks[-2], peaks[-1]).astype(jnp.bfloat16).astype(jnp.float32)
            scales = [jnp.exp2(p - top) for p in peaks[-2:]]
            total = totals[-2] * scales[0] + totals[-1] * scales[1]
            spans = [slice(h * rows, (h + 1) * rows) for h in range(heads)]
            for h, span in enumerate(spans):
                value = acc[0, :, span] * scales[0][:, span] + acc[1, :, span] * scales[1][:, span]
                outs[i][h * HEAD : (h + 1) * HEAD, :] = value.astype(jnp.bfloat16)
            outs[i][heads * HEAD :, :] = pack_stats(
                [top[:, span] for span in spans], [total[:, span] for span in spans]
            )


def attend(q_blocks, order, groups, kv, kv_far, keep, heads, tile=256):
    count = groups.shape[0]
    n_blocks = len(q_blocks)
    block_rows = q_blocks[0].shape[0]
    rows = block_rows * n_blocks
    ctx = kv.shape[1]
    width = heads * HEAD
    length = width + STAT_ROWS
    return pl.pallas_call(
        lambda *refs: attend_kernel(heads, tile, *refs),
        grid_spec=pltpu.PrefetchScalarGridSpec(
            num_scalar_prefetch=2,
            grid=(1,),
            in_specs=[
                pl.BlockSpec((block_rows, width), lambda z, o, g, i=i: (0, g[i]))
                for i in range(count)
                for _ in q_blocks
            ]
            + [pl.BlockSpec(memory_space=pl.ANY)] * 2
            + [pl.BlockSpec(keep.shape, lambda z, o, g: (0, 0))],
            out_specs=[pl.BlockSpec((length, rows), lambda z, o, g: (0, 0)) for _ in range(count)],
            scratch_shapes=[
                pltpu.VMEM((4 * count, ctx, HEAD), jnp.bfloat16),
                pltpu.VMEM((count, heads, n_blocks, block_rows, HEAD), jnp.bfloat16),
                pltpu.VMEM((2, ctx, heads * rows), jnp.float32),
                pltpu.VMEM((2, HEAD, heads * rows), jnp.float32),
                pltpu.SemaphoreType.DMA((4 * count,)),
            ],
        ),
        out_shape=[jax.ShapeDtypeStruct((length, rows), jnp.bfloat16) for _ in range(count)],
        compiler_params=pltpu.CompilerParams(
            dimension_semantics=("arbitrary",), vmem_limit_bytes=ATTEND_VMEM
        ),
        cost_estimate=pl.CostEstimate(
            flops=12 * count * rows * width * 2 * ctx,
            bytes_accessed=8 * count * ctx * HEAD,
            transcendentals=count * rows * heads * 2 * ctx,
        ),
        name="attend",
    )(order, groups, *(list(q_blocks) * count), kv, kv_far, keep)


def merge_parts(parts, heads):
    stats = [unpack_stats(p[heads * HEAD :, :], heads) for p in parts]
    top = stats[0][0]
    for peaks, _ in stats[1:]:
        top = jnp.maximum(top, peaks)
    scales = [jnp.exp2(peaks - top) for peaks, _ in stats]
    total = sum(w * t for w, (_, t) in zip(scales, stats))
    values = []
    for h in range(heads):
        place = slice(h * HEAD, (h + 1) * HEAD)
        values.append(
            sum(w[h : h + 1] * p[place, :].astype(jnp.float32) for w, p in zip(scales, parts))
        )
    return top, total, values


def merge_kernel(heads, pairs, *refs):
    for p in range(pairs):
        near, came, out = refs[2 * p], refs[2 * p + 1], refs[2 * pairs + p]
        top, total, values = merge_parts([near, came], heads)
        for h in range(heads):
            out[h * HEAD : (h + 1) * HEAD, :] = values[h].astype(jnp.bfloat16)
        rows = [slice(h, h + 1) for h in range(heads)]
        out[heads * HEAD :, :] = pack_stats([top[r] for r in rows], [total[r] for r in rows])


def merge(pairs, heads):
    shape = pairs[0][0].shape
    spec = pl.BlockSpec(shape, lambda: (0, 0))
    return pl.pallas_call(
        lambda *refs: merge_kernel(heads, len(pairs), *refs),
        in_specs=[spec] * (2 * len(pairs)),
        out_specs=[spec] * len(pairs),
        out_shape=[jax.ShapeDtypeStruct(shape, jnp.bfloat16)] * len(pairs),
        compiler_params=pltpu.CompilerParams(vmem_limit_bytes=ATTEND_VMEM),
        cost_estimate=pl.CostEstimate(
            flops=1000000, bytes_accessed=6 * shape[0] * shape[1] * len(pairs), transcendentals=0
        ),
        name="merge",
    )(*[x for pair in pairs for x in pair])


def project_kernel(heads, core, *refs):
    parts, (w_ref, kept, sent, attended) = refs[:-4], refs[-4:]

    @pl.when(pl.program_id(0) == 0)
    def _():
        _, total, values = merge_parts(parts, heads)
        for h in range(heads):
            mean = values[h] / total[h : h + 1]
            attended[:, h * HEAD : (h + 1) * HEAD] = mean.T.astype(jnp.bfloat16)

    full = jnp.dot(attended[...], w_ref[...], preferred_element_type=jnp.float32)
    chips, per_dev, tile = kept.shape
    full = full.reshape(chips, 2, per_dev, tile)
    first = core[0] == 0
    kept[...] = jnp.where(first, full[:, 0], full[:, 1])
    away = jnp.where(first, full[:, 1], full[:, 0])
    sent[...] = away.reshape(chips * per_dev, tile).astype(jnp.bfloat16)


def project(parts, core, w_out, heads, per_dev, part, part_count, tile=1024):
    length, rows = parts[0].shape
    chips = rows // (2 * per_dev)
    cols = w_out.shape[1] // part_count
    steps = cols // tile
    return pl.pallas_call(
        lambda *refs: project_kernel(heads, *refs),
        grid_spec=pltpu.PrefetchScalarGridSpec(
            num_scalar_prefetch=1,
            grid=(steps,),
            in_specs=[pl.BlockSpec((length, rows), lambda j, c: (0, 0)) for _ in parts]
            + [pl.BlockSpec((heads * HEAD, tile), lambda j, c: (0, j + part * steps))],
            out_specs=[
                pl.BlockSpec((chips, per_dev, tile), lambda j, c: (0, 0, j)),
                pl.BlockSpec((chips * per_dev, tile), lambda j, c: (0, j)),
            ],
            scratch_shapes=[pltpu.VMEM((rows, heads * HEAD), jnp.bfloat16)],
        ),
        out_shape=[
            jax.ShapeDtypeStruct((chips, per_dev, cols), jnp.float32),
            jax.ShapeDtypeStruct((chips * per_dev, cols), jnp.bfloat16),
        ],
        compiler_params=pltpu.CompilerParams(dimension_semantics=("arbitrary",)),
        cost_estimate=pl.CostEstimate(
            flops=2 * rows * heads * HEAD * cols,
            bytes_accessed=3 * heads * HEAD * cols,
            transcendentals=0,
        ),
        name="project",
    )(core, *parts, w_out)


def paired_device(queries, steer_ids, steer_table, kv, blocks, w_out):
    n = lax.axis_size("ctx")
    me = lax.axis_index("ctx")
    chips = n // 2
    core = me % 2
    chip = me // 2
    per_dev = queries.shape[0]
    rows = per_dev * n
    width = D // n
    heads = width // HEAD
    swap = [(i, i ^ 1) for i in range(n)]
    ring = list(range(0, chips, 2)) + list(range(chips - 1, 0, -2))

    def hop(step):
        return [
            (2 * ring[p] + c, 2 * ring[(p + step) % chips] + c) for p in range(chips) for c in range(2)
        ]

    ahead_pairs, behind_pairs = hop(1), hop(-1)
    place = jnp.where(chip % 2 == 0, chip // 2, chips - 1 - chip // 2)

    def chip_at(offset):
        p = (place + offset) % chips
        return jnp.where(p < chips // 2, 2 * p, 2 * (chips - 1 - p) + 1)

    steered = apply_steer(queries, steer_ids, steer_table)
    halves = steered.reshape(per_dev, chips, 2, width)
    mine = jnp.where(core == 0, halves[:, :, 0], halves[:, :, 1]).reshape(per_dev, D // 2)
    other = jnp.where(core == 0, halves[:, :, 1], halves[:, :, 0]).reshape(per_dev, D // 2)
    theirs = lax.ppermute(other, "ctx", swap)
    block = jnp.concatenate(
        [jnp.where(core == 0, mine, theirs), jnp.where(core == 0, theirs, mine)], axis=0
    )
    found, offsets = [block], [0]
    ahead, behind = block, block
    for s in range(1, chips // 2 + 1):
        ahead = lax.ppermute(ahead, "ctx", ahead_pairs)
        found.append(ahead)
        offsets.append(-s)
        if s < chips - s:
            behind = lax.ppermute(behind, "ctx", behind_pairs)
            found.append(behind)
            offsets.append(s)
        if s == 1:
            ahead, kv_late, blocks_late = lax.optimization_barrier((ahead, kv, blocks))
            kv_far = lax.ppermute(kv_late, "ctx", swap)
    order = chip_at(jnp.array(offsets, jnp.int32))

    block_count = kv.shape[1] // BLOCK
    ids = jnp.arange(2 * block_count, dtype=jnp.int32)
    ids = jnp.where(ids < block_count, me * block_count + ids, (me ^ 1) * block_count + ids - block_count)
    hits = jnp.any(blocks_late[:, None, :] == ids[None, :, None], axis=2)
    keep = jnp.repeat(hits.T.astype(jnp.float32), BLOCK, axis=1)
    keep = jnp.concatenate([keep] * heads, axis=1)

    half = chips // 2

    def attend_for(targets):
        groups = chip_at(jnp.array(targets, jnp.int32))
        return attend(found, order, groups, kv, kv_far, keep, heads)

    went_ahead, went_behind = None, None
    for s in range(1, half + 1):
        outs = attend_for([half + 1 - s] + ([s - 1 - half] if s > 1 else []))
        came = [went_ahead, went_behind]
        pairs = [(x, y) for x, y in zip(outs, came) if y is not None]
        if pairs:
            merged = merge(pairs, heads)
            outs = list(merged) + list(outs[len(merged) :])
        went_ahead = lax.ppermute(outs[0], "ctx", ahead_pairs)
        if s > 1:
            went_behind = lax.ppermute(outs[1], "ctx", behind_pairs)
    parts = [attend_for([0])[0], went_ahead, went_behind]

    col_parts = 2
    pieces = []
    for h in range(col_parts):
        kept, sent = project(parts, core.reshape(1), w_out, heads, per_dev, h, col_parts)
        got = lax.ppermute(sent, "ctx", swap).reshape(kept.shape)
        pieces.append((kept, got))

    def term(piece, offset):
        at = chip_at(offset)
        pick = [lax.dynamic_index_in_dim(x, at, 0, keepdims=False) for x in piece]
        return pick[0] + pick[1].astype(jnp.float32)

    streams = [[None, None] for _ in pieces]
    for s in range(1, half + 1):
        for h, piece in enumerate(pieces):
            came_ahead, came_behind = streams[h]
            total = term(piece, half + 1 - s)
            if came_ahead is not None:
                total = total + came_ahead.astype(jnp.float32)
            streams[h][0] = lax.ppermute(total.astype(jnp.bfloat16), "ctx", ahead_pairs)
            if s > 1:
                total = term(piece, s - 1 - half)
                if came_behind is not None:
                    total = total + came_behind.astype(jnp.float32)
                streams[h][1] = lax.ppermute(total.astype(jnp.bfloat16), "ctx", behind_pairs)
    done = []
    for piece, (came_ahead, came_behind) in zip(pieces, streams):
        total = term(piece, 0) + came_ahead.astype(jnp.float32) + came_behind.astype(jnp.float32)
        done.append(total.astype(jnp.bfloat16))
    return jnp.concatenate(done, axis=1)


def solution(mesh):
    n = mesh.shape["ctx"]
    paired = n == 2 * KV_HEADS
    return jax.shard_map(
        paired_device if paired else per_device,
        mesh=mesh,
        in_specs=(
            P(("parts", "ctx"), None),
            P(("parts", "ctx")),
            P(),
            P(None, ("parts", "ctx"), None),
            P("parts", None),
            P("ctx", None),
        ),
        out_specs=P(("parts", "ctx"), None),
        check_vma=False,
    )
```

```python
import jax
import jax.numpy as jnp
from jax import lax
from jax.experimental import pallas as pl
from jax.experimental.pallas import tpu as pltpu
from jax.sharding import PartitionSpec as P

HEADS = 64
KV_HEADS = 8
HEAD = 128
D = 8192
BLOCK = 64


def apply_steer(queries, steer_ids, steer_table):
    lookup_ids = jnp.arange(steer_table.shape[0], dtype=jnp.int32)
    one_hot = (steer_ids[:, None] == lookup_ids[None, :]).astype(jnp.bfloat16)
    lookup = jnp.dot(one_hot, steer_table, preferred_element_type=jnp.float32)
    return (queries.astype(jnp.float32) + lookup).astype(jnp.bfloat16)


def local_keep(blocks, first_block, block_count, query_count):
    block_ids = first_block + jnp.arange(block_count, dtype=jnp.int32)
    hits = jnp.any(blocks[:, :, None] == block_ids[None, None, :], axis=1)
    full = jnp.broadcast_to(
        hits[:, None, :, None], (query_count // BLOCK, BLOCK, block_count, BLOCK)
    )
    return full.reshape(query_count, block_count * BLOCK)


def group_attend(q_rows, k_rows, v_rows, keep_rows):
    scores = lax.dot_general(
        q_rows, k_rows, (((1,), (1,)), ((), ())), preferred_element_type=jnp.float32
    )
    scores = scores * HEAD ** (-0.5)
    masked = jnp.where(keep_rows, scores, jnp.float32(-1e30))
    row_peak = jnp.max(masked, axis=1)
    weights = jnp.where(keep_rows, jnp.exp(masked - row_peak[:, None]), jnp.float32(0.0))
    row_total = jnp.sum(weights, axis=1)
    probs = weights.astype(jnp.bfloat16)
    partial_out = jnp.dot(probs, v_rows, preferred_element_type=jnp.float32)
    return (row_peak, row_total, partial_out)


def partial_attention(steered, kv_piece, keep_mask):
    query_count = steered.shape[0]
    ctx_count = kv_piece.shape[1]
    group_size = HEADS // KV_HEADS
    q_groups = steered.reshape(query_count, KV_HEADS, group_size, HEAD).transpose(1, 2, 0, 3)
    q_groups = q_groups.reshape(KV_HEADS, group_size * query_count, HEAD)
    k_groups = kv_piece[0].reshape(ctx_count, KV_HEADS, HEAD).transpose(1, 0, 2)
    v_groups = kv_piece[1].reshape(ctx_count, KV_HEADS, HEAD).transpose(1, 0, 2)
    keep_rows = jnp.tile(keep_mask, (group_size, 1))

    def one_group(triple):
        return group_attend(triple[0], triple[1], triple[2], keep_rows)

    peaks, totals, outs = lax.map(one_group, (q_groups, k_groups, v_groups))
    peaks = (
        peaks.reshape(KV_HEADS, group_size, query_count)
        .transpose(2, 0, 1)
        .reshape(query_count, HEADS)
    )
    totals = (
        totals.reshape(KV_HEADS, group_size, query_count)
        .transpose(2, 0, 1)
        .reshape(query_count, HEADS)
    )
    outs = (
        outs.reshape(KV_HEADS, group_size, query_count, HEAD)
        .transpose(2, 0, 1, 3)
        .reshape(query_count, HEADS * HEAD)
    )
    return (peaks, totals, outs)


def per_device(queries, steer_ids, steer_table, kv, blocks, w_out):
    steered_local = apply_steer(queries, steer_ids, steer_table)
    steered = lax.all_gather(steered_local, "ctx", axis=0, tiled=True)
    shard_count = lax.axis_size("ctx")
    my_index = lax.axis_index("ctx")
    query_count = steered.shape[0]
    block_count = kv.shape[1] // BLOCK
    keep_mask = local_keep(blocks, my_index * block_count, block_count, query_count)
    peaks, totals, outs = partial_attention(steered, kv, keep_mask)
    stat_width = max(HEADS, shard_count)
    per_entry = D // stat_width
    col_count = D // shard_count

    def spread(values):
        return jnp.repeat(values, stat_width // HEADS, axis=1)

    got_num, got_max, got_den = (
        lax.all_to_all(outs, "ctx", split_axis=1, concat_axis=0, tiled=True),
        lax.all_to_all(spread(peaks), "ctx", split_axis=1, concat_axis=0, tiled=True),
        lax.all_to_all(spread(totals), "ctx", split_axis=1, concat_axis=0, tiled=True),
    )
    got_num = got_num.reshape(shard_count, query_count, col_count)
    got_max = got_max.reshape(shard_count, query_count, stat_width // shard_count)
    got_den = got_den.reshape(shard_count, query_count, stat_width // shard_count)
    overall = jnp.max(got_max, axis=0)
    scales = jnp.exp(got_max - overall[None])
    denominator = jnp.sum(scales * got_den, axis=0)
    numerator = jnp.sum(jnp.repeat(scales, per_entry, axis=2) * got_num, axis=0)
    attended = (numerator / jnp.repeat(denominator, per_entry, axis=1)).astype(jnp.bfloat16)
    return lax.psum_scatter(
        jnp.dot(attended, w_out, preferred_element_type=jnp.float32),
        "ctx",
        scatter_dimension=0,
        tiled=True,
    ).astype(jnp.bfloat16)


NONE = -(2.0**100)
LOG2E = 1.4426950408889634
STAT_ROWS = 16
ATTEND_VMEM = 16 * 1024 * 1024
SMALL_VMEM = 4 * 1024 * 1024


def pack_stats(peaks, totals):
    high = [t.astype(jnp.bfloat16).astype(jnp.float32) for t in totals]
    flat = peaks + high + [t - h for t, h in zip(totals, high)]
    flat += [jnp.zeros_like(flat[0])] * (STAT_ROWS - len(flat))
    return jnp.concatenate(flat, axis=0).astype(jnp.bfloat16)


def unpack_stats(stats, heads):
    stats = stats.astype(jnp.float32)
    return stats[:heads], stats[heads : 2 * heads] + stats[2 * heads : 3 * heads]


def ring_chip(position, chips):
    return jnp.where(position < chips // 2, 2 * position, 2 * (chips - 1 - position) + 1)


def ring_place(chip, chips):
    return jnp.where(chip % 2 == 0, chip // 2, chips - 1 - chip // 2)


def near_chip(place, offset, chips):
    position = place + (offset + chips) % chips
    return ring_chip(jnp.where(position >= chips, position - chips, position), chips)


def attend_kernel(heads, tile, offsets, targets, *refs):
    n_blocks, count = len(offsets), len(targets)
    q_blocks = refs[:n_blocks]
    sources = refs[n_blocks : n_blocks + 2]
    keep = refs[n_blocks + 2]
    outs = refs[n_blocks + 3 : n_blocks + 3 + count]
    q_all, scores, acc = refs[n_blocks + 3 + count :]
    block_rows = q_blocks[0].shape[0]
    rows = n_blocks * block_rows
    lanes = heads * rows
    ctx = sources[0].shape[1]
    key_blocks, per_tile = ctx // BLOCK, tile // BLOCK
    to_log2 = HEAD ** (-0.5) * LOG2E
    units = [(i, s) for i in range(count) for s in range(2)]
    place = ring_place(lax.axis_index("ctx") // 2, n_blocks)
    order = [near_chip(place, d, n_blocks) for d in offsets]
    groups = [near_chip(place, d, n_blocks) for d in targets]

    def load(u, kind, t):
        i, s = units[u]
        column = pl.ds(pl.multiple_of(groups[i] * HEAD, HEAD), HEAD)
        return sources[s][kind, t * tile : (t + 1) * tile, column]

    for i in range(count):
        for at in range(n_blocks):
            for h in range(heads):
                column = pl.ds(pl.multiple_of((groups[i] * heads + h) * HEAD, HEAD), HEAD)
                q_all[i, h, order[at]] = q_blocks[at][:, column]

    def score(u, t, peak):
        i, s = units[u]
        piece = lax.dot_general(
            load(u, 0, t),
            q_all[i].reshape(lanes, HEAD),
            (((1,), (1,)), ((), ())),
            preferred_element_type=jnp.float32,
        )
        scores[u % 2, t * tile : (t + 1) * tile, :] = piece
        for b in range(per_tile):
            kept = keep[pl.ds(s * key_blocks + t * per_tile + b, 1), :]
            part = piece[b * BLOCK : (b + 1) * BLOCK, :].reshape(BLOCK // 8, 8, lanes)
            best = jnp.max(part, axis=0) * to_log2
            peak = jnp.maximum(peak, jnp.where(kept > 0.0, best, NONE))
        return peak

    def weigh(u, t, peak, total):
        s = units[u][1]
        probs = []
        for b in range(per_tile):
            kept = keep[pl.ds(s * key_blocks + t * per_tile + b, 1), :]
            shift = jnp.where(kept > 0.0, peak, -NONE)
            low = t * tile + b * BLOCK
            weights = jnp.exp2(scores[u % 2, low : low + BLOCK, :] * to_log2 - shift)
            total = total + jnp.sum(weights.reshape(BLOCK // 8, 8, lanes), axis=0)
            probs.append(weights.astype(jnp.bfloat16))
        fresh = jnp.dot(
            load(u, 1, t).T,
            jnp.concatenate(probs, axis=0),
            preferred_element_type=jnp.float32,
        )
        acc[s] = fresh if t == 0 else acc[s] + fresh
        return total

    tiles = range(ctx // tile)
    lowest = jnp.full((8, lanes), NONE, jnp.float32)
    peak = lowest
    for t in tiles:
        peak = score(0, t, peak)
    peaks, totals = [], []
    for u, (i, s) in enumerate(units):
        row = jnp.max(peak, axis=0, keepdims=True)
        total = jnp.zeros((8, lanes), jnp.float32)
        peak = lowest
        for t in tiles:
            if u + 1 < len(units):
                peak = score(u + 1, t, peak)
            total = weigh(u, t, row, total)
        peaks.append(row)
        totals.append(jnp.sum(total, axis=0, keepdims=True))
        if s == 1:
            top = jnp.maximum(peaks[-2], peaks[-1]).astype(jnp.bfloat16).astype(jnp.float32)
            scales = [jnp.exp2(p - top) for p in peaks[-2:]]
            total = totals[-2] * scales[0] + totals[-1] * scales[1]
            spans = [slice(h * rows, (h + 1) * rows) for h in range(heads)]
            for h, span in enumerate(spans):
                value = acc[0, :, span] * scales[0][:, span] + acc[1, :, span] * scales[1][:, span]
                outs[i][h * HEAD : (h + 1) * HEAD, :] = value.astype(jnp.bfloat16)
            outs[i][heads * HEAD :, :] = pack_stats(
                [top[:, span] for span in spans], [total[:, span] for span in spans]
            )


def in_vmem(x):
    return pltpu.with_memory_space_constraint(x, pltpu.VMEM)


def attend(q_blocks, offsets, targets, kv, kv_far, keep, heads, tile=256):
    count, n_blocks = len(targets), len(q_blocks)
    block_rows = q_blocks[0].shape[0]
    rows = block_rows * n_blocks
    ctx = kv.shape[1]
    width = heads * HEAD
    length = width + STAT_ROWS
    whole = pl.BlockSpec(memory_space=pltpu.VMEM)
    return pl.pallas_call(
        lambda *refs: attend_kernel(heads, tile, offsets, targets, *refs),
        in_specs=[whole] * (n_blocks + 3),
        out_specs=[whole] * count,
        scratch_shapes=[
            pltpu.VMEM((count, heads, n_blocks, block_rows, HEAD), jnp.bfloat16),
            pltpu.VMEM((2, ctx, heads * rows), jnp.float32),
            pltpu.VMEM((2, HEAD, heads * rows), jnp.float32),
        ],
        out_shape=[pltpu.VMEM((length, rows), jnp.bfloat16) for _ in range(count)],
        compiler_params=pltpu.CompilerParams(vmem_limit_bytes=ATTEND_VMEM),
        cost_estimate=pl.CostEstimate(
            flops=12 * count * rows * width * 2 * ctx,
            bytes_accessed=8 * count * ctx * HEAD,
            transcendentals=count * rows * heads * 2 * ctx,
        ),
        name="attend",
    )(*[in_vmem(x) for x in q_blocks], in_vmem(kv), in_vmem(kv_far), in_vmem(keep))


def merge_parts(parts, heads):
    stats = [unpack_stats(p[heads * HEAD :, :], heads) for p in parts]
    top = stats[0][0]
    for peaks, _ in stats[1:]:
        top = jnp.maximum(top, peaks)
    scales = [jnp.exp2(peaks - top) for peaks, _ in stats]
    total = sum(w * t for w, (_, t) in zip(scales, stats))
    values = []
    for h in range(heads):
        place = slice(h * HEAD, (h + 1) * HEAD)
        values.append(
            sum(w[h : h + 1] * p[place, :].astype(jnp.float32) for w, p in zip(scales, parts))
        )
    return top, total, values


def merge_kernel(heads, pairs, *refs):
    for p in range(pairs):
        near, came, out = refs[2 * p], refs[2 * p + 1], refs[2 * pairs + p]
        top, total, values = merge_parts([near, came], heads)
        for h in range(heads):
            out[h * HEAD : (h + 1) * HEAD, :] = values[h].astype(jnp.bfloat16)
        rows = [slice(h, h + 1) for h in range(heads)]
        out[heads * HEAD :, :] = pack_stats([top[r] for r in rows], [total[r] for r in rows])


def merge(pairs, heads):
    shape = pairs[0][0].shape
    whole = pl.BlockSpec(memory_space=pltpu.VMEM)
    return pl.pallas_call(
        lambda *refs: merge_kernel(heads, len(pairs), *refs),
        in_specs=[whole] * (2 * len(pairs)),
        out_specs=[whole] * len(pairs),
        out_shape=[pltpu.VMEM(shape, jnp.bfloat16)] * len(pairs),
        compiler_params=pltpu.CompilerParams(vmem_limit_bytes=SMALL_VMEM),
        cost_estimate=pl.CostEstimate(
            flops=1000000, bytes_accessed=6 * shape[0] * shape[1] * len(pairs), transcendentals=0
        ),
        name="merge",
    )(*[in_vmem(x) for pair in pairs for x in pair])


def finish_kernel(heads, *refs):
    parts, attended = refs[:-1], refs[-1]
    _, total, values = merge_parts(parts, heads)
    for h in range(heads):
        mean = values[h] / total[h : h + 1]
        attended[:, h * HEAD : (h + 1) * HEAD] = mean.T.astype(jnp.bfloat16)


def finish(parts, heads):
    length, rows = parts[0].shape
    whole = pl.BlockSpec(memory_space=pltpu.VMEM)
    return pl.pallas_call(
        lambda *refs: finish_kernel(heads, *refs),
        in_specs=[whole] * len(parts),
        out_specs=whole,
        out_shape=pltpu.VMEM((rows, heads * HEAD), jnp.bfloat16),
        compiler_params=pltpu.CompilerParams(vmem_limit_bytes=SMALL_VMEM),
        cost_estimate=pl.CostEstimate(
            flops=1000000, bytes_accessed=2 * length * rows * len(parts), transcendentals=0
        ),
        name="finish",
    )(*[in_vmem(x) for x in parts])


def project_kernel(low, tile, attended, w_ref, kept, sent):
    chips, per_dev, cols = kept.shape
    first = lax.axis_index("ctx") % 2 == 0
    for j in range(cols // tile):
        span = slice(j * tile, (j + 1) * tile)
        full = jnp.dot(
            attended[...],
            w_ref[:, low + j * tile : low + (j + 1) * tile],
            preferred_element_type=jnp.float32,
        )
        full = full.reshape(chips, 2, per_dev, tile)
        kept[:, :, span] = jnp.where(first, full[:, 0], full[:, 1])
        away = jnp.where(first, full[:, 1], full[:, 0])
        sent[:, :, span] = away.astype(jnp.bfloat16)


def project(attended, w_out, per_dev, part, part_count, tile=512):
    rows, width = attended.shape
    chips = rows // (2 * per_dev)
    cols = w_out.shape[1] // part_count
    whole = pl.BlockSpec(memory_space=pltpu.VMEM)
    return pl.pallas_call(
        lambda *refs: project_kernel(part * cols, tile, *refs),
        in_specs=[whole] * 2,
        out_specs=[whole] * 2,
        out_shape=[
            pltpu.VMEM((chips, per_dev, cols), jnp.float32),
            pltpu.VMEM((chips, per_dev, cols), jnp.bfloat16),
        ],
        compiler_params=pltpu.CompilerParams(vmem_limit_bytes=SMALL_VMEM),
        cost_estimate=pl.CostEstimate(
            flops=2 * rows * width * cols, bytes_accessed=3 * width * cols, transcendentals=0
        ),
        name="project",
    )(in_vmem(attended), in_vmem(w_out))


def fold_kernel(targets, pieces, refs_per, *refs):
    terms = refs[: 2 * pieces]
    came = refs[2 * pieces : len(refs) - len(targets)]
    outs = refs[len(refs) - len(targets) :]
    chips, _, cols = terms[0].shape
    place = ring_place(lax.axis_index("ctx") // 2, chips)
    for i, target in enumerate(targets):
        chip = near_chip(place, target, chips)
        mine = came[i * refs_per : (i + 1) * refs_per]
        for h in range(pieces):
            span = slice(h * cols, (h + 1) * cols)
            total = terms[2 * h][chip] + terms[2 * h + 1][chip].astype(jnp.float32)
            for ref in mine:
                total = total + ref[:, span].astype(jnp.float32)
            outs[i][:, span] = total.astype(jnp.bfloat16)


def fold(targets, terms, came, last=False):
    _, per_dev, cols = terms[0].shape
    shape = (per_dev, cols * len(terms) // 2)
    whole = pl.BlockSpec(memory_space=pltpu.VMEM)
    made = jax.ShapeDtypeStruct(shape, jnp.bfloat16) if last else pltpu.VMEM(shape, jnp.bfloat16)
    return pl.pallas_call(
        lambda *refs: fold_kernel(targets, len(terms) // 2, len(came) // len(targets), *refs),
        in_specs=[whole] * (len(terms) + len(came)),
        out_specs=[whole] * len(targets),
        out_shape=[made] * len(targets),
        compiler_params=pltpu.CompilerParams(vmem_limit_bytes=SMALL_VMEM),
        cost_estimate=pl.CostEstimate(
            flops=1000000, bytes_accessed=20 * per_dev * cols * len(targets), transcendentals=0
        ),
        name="fold",
    )(*[in_vmem(x) for x in list(terms) + list(came)])


def stage_kernel(source, held, done):
    copy = pltpu.make_async_copy(source, held, done)
    copy.start()
    copy.wait()


def stage(x):
    return pl.pallas_call(
        stage_kernel,
        in_specs=[pl.BlockSpec(memory_space=pl.ANY)],
        out_specs=pl.BlockSpec(memory_space=pltpu.VMEM),
        out_shape=pltpu.VMEM(x.shape, x.dtype),
        scratch_shapes=[pltpu.SemaphoreType.DMA],
        compiler_params=pltpu.CompilerParams(vmem_limit_bytes=SMALL_VMEM),
        cost_estimate=pl.CostEstimate(
            flops=0, bytes_accessed=2 * x.size * x.dtype.itemsize, transcendentals=0
        ),
        name="stage",
    )(x)


def paired_device(queries, steer_ids, steer_table, kv, blocks, w_out):
    n = lax.axis_size("ctx")
    me = lax.axis_index("ctx")
    chips = n // 2
    core = me % 2
    chip = me // 2
    per_dev = queries.shape[0]
    rows = per_dev * n
    width = D // n
    heads = width // HEAD
    swap = [(i, i ^ 1) for i in range(n)]
    ring = list(range(0, chips, 2)) + list(range(chips - 1, 0, -2))

    def hop(step):
        return [
            (2 * ring[p] + c, 2 * ring[(p + step) % chips] + c) for p in range(chips) for c in range(2)
        ]

    ahead_pairs, behind_pairs = hop(1), hop(-1)
    steered = apply_steer(queries, steer_ids, steer_table)
    halves = steered.reshape(per_dev, chips, 2, width)
    mine = jnp.where(core == 0, halves[:, :, 0], halves[:, :, 1]).reshape(per_dev, D // 2)
    other = jnp.where(core == 0, halves[:, :, 1], halves[:, :, 0]).reshape(per_dev, D // 2)
    theirs = lax.ppermute(other, "ctx", swap)
    block = jnp.concatenate(
        [jnp.where(core == 0, mine, theirs), jnp.where(core == 0, theirs, mine)], axis=0
    )
    half = chips // 2
    far_pairs = hop(half)
    found, offsets = [block], [0]
    ahead, behind, far = block, block, None
    for s in range(1, half):
        ahead = lax.ppermute(ahead, "ctx", ahead_pairs)
        behind = lax.ppermute(behind, "ctx", behind_pairs)
        if s == 1:
            far = lax.ppermute(block, "ctx", far_pairs)
            ahead, kv_late, blocks_late = lax.optimization_barrier((ahead, kv, blocks))
            kv_far = lax.ppermute(kv_late, "ctx", swap)
        found += [ahead, behind]
        offsets += [-s, s]
    found.append(far)
    offsets.append(half)

    block_count = kv.shape[1] // BLOCK
    ids = jnp.arange(2 * block_count, dtype=jnp.int32)
    ids = jnp.where(ids < block_count, me * block_count + ids, (me ^ 1) * block_count + ids - block_count)
    hits = jnp.any(blocks_late[:, None, :] == ids[None, :, None], axis=2)
    keep = jnp.repeat(hits.T.astype(jnp.float32), BLOCK, axis=1)
    keep = jnp.concatenate([keep] * heads, axis=1)

    kv_near = stage(kv_late)

    def attend_for(targets):
        return attend(found, offsets, targets, kv_near, kv_far, keep, heads)

    went_ahead, went_behind, went_far = None, None, None
    for s in range(1, half):
        targets = [half - s, s - half]
        if s == 1:
            outs = attend_for(targets + [half])
            last = outs[2]
        else:
            outs = merge(list(zip(attend_for(targets), [went_ahead, went_behind])), heads)
        went_ahead = lax.ppermute(outs[0], "ctx", ahead_pairs)
        went_behind = lax.ppermute(outs[1], "ctx", behind_pairs)
        if s == 1:
            went_far = lax.ppermute(last, "ctx", far_pairs)
    parts = [attend_for([0])[0], went_ahead, went_behind, went_far]

    attended = finish(parts, heads)
    col_parts = 2
    terms = []
    for h in range(col_parts):
        kept, sent = project(attended, w_out, per_dev, h, col_parts)
        terms += [kept, lax.ppermute(sent, "ctx", swap)]
    went_ahead, went_behind, went_far = None, None, None
    for s in range(1, half):
        came = [] if s == 1 else [went_ahead, went_behind]
        outs = fold([half - s, s - half] + ([half] if s == 1 else []), terms, came)
        went_ahead = lax.ppermute(outs[0], "ctx", ahead_pairs)
        went_behind = lax.ppermute(outs[1], "ctx", behind_pairs)
        if s == 1:
            went_far = lax.ppermute(outs[2], "ctx", far_pairs)
    return fold([0], terms, [went_ahead, went_behind, went_far], last=True)[0]


def solution(mesh):
    n = mesh.shape["ctx"]
    paired = n == 2 * KV_HEADS
    return jax.shard_map(
        paired_device if paired else per_device,
        mesh=mesh,
        in_specs=(
            P(("parts", "ctx"), None),
            P(("parts", "ctx")),
            P(),
            P(None, ("parts", "ctx"), None),
            P("parts", None),
            P("ctx", None),
        ),
        out_specs=P(("parts", "ctx"), None),
        check_vma=False,
    )
```
